256 devices in a mesh: box: 16 (over z, x_lo), dir: 16 (over x_hi, y, core).
Axes of the slice: x: 4 (x_hi: 2, x_lo: 2; x = x_hi * 2 + x_lo), y: 4, z: 8, core: 2. Of those that a mesh axis runs over, the one named last changes fastest.
Arguments:
- fine_out: bfloat16 [4096, 32, 512], P(('box', 'dir')), may hold values from -6 to 6
- fine_list: int32 [4096, 12], P(('box', 'dir')), may hold values from -1 to 4095, as said below
- fine_slot: int32 [4096], P('box'), may hold values from 0 to 3, as said below
- fine_translator: float32 [12, 2, 512], replicated, may hold values from -4 to 4
- theta_up_fine: bfloat16 [32, 16], replicated, may hold values from -1.5 to 1.5
- phi_up_fine: bfloat16 [64, 32], replicated, may hold values from -1 to 1
- middle_phase: float32 [4, 2048], replicated, may hold values from -3.140625 to 3.140625
- middle_list: int32 [1024, 12], P('box'), may hold values from -1 to 1023, as said below
- middle_slot: int32 [1024], P('box'), may hold values from 0 to 3, as said below
- middle_translator: float32 [12, 2, 2048], P(None, None, 'dir'), may hold values from -2 to 2
- theta_up_middle: bfloat16 [64, 32], replicated, may hold values from -1 to 1
- phi_up_middle: bfloat16 [128, 64], replicated, may hold values from -0.75 to 0.75
- coarse_phase: float32 [4, 8192], replicated, may hold values from -3.140625 to 3.140625
- coarse_list: int32 [256, 12], replicated, may hold values from -1 to 255, as said below
- coarse_translator: float32 [12, 2, 8192], P(None, None, ('box', 'dir')), may hold values from -1.25 to 1.25
Outputs:
- fine_in: bfloat16 [4096, 32, 512], P(('box', 'dir'))
- middle_in: bfloat16 [1024, 32, 2048], P('box', None, 'dir')
- coarse_in: bfloat16 [256, 32, 8192], P(None, None, ('box', 'dir'))
The draws below stay inside these ranges and needn't reach their ends.
Inputs may be any that keep to these rules, and one draw needn't show every extreme that they name: `fine_list`: row i names distinct fine boxes j with 2 <= |j - i| <= 7 and |j // 4 - i // 4| <= 1, in any slots; -1 marks an empty slot. `middle_list`: row i names distinct middle boxes j with 2 <= |j - i| <= 7 and |j // 4 - i // 4| <= 1, in any slots; -1 marks an empty slot. `coarse_list`: row i names distinct coarse boxes j with 2 <= |j - i| <= 7 and |j // 4 - i // 4| <= 1, in any slots; -1 marks an empty slot. `fine_slot`: the parent of fine box c is middle box c // 4; each aligned group of 4 fine boxes takes each of the values 0 to 3 once. `middle_slot`: the parent of middle box m is coarse box m // 4; each aligned group of 4 middle boxes takes each of the values 0 to 3 once.
All inputs are finite; a program needn't handle non-finite values.
Results may differ from the reference program's by a relative error of at most 0.007.
Values may be sent and summed in bfloat16 or wider, within the bound.
No kernel may reach another device: no remote copies, remote signals or barrier semaphores. Data moves between devices by JAX's collectives and lax.ppermute only.
A program may use at most 64 MiB of HBM per device.

```python
import jax
import jax.numpy as jnp
from jax import lax

MAX_OFFSET = 7
THETA_FINE = 16
PHI_FINE = 32
THETA_MID = 32
PHI_MID = 64
THETA_COARSE = 64
PHI_COARSE = 128
COMPONENTS = 32
LIST_SLOTS = 12
DIRS_FINE = 512
DIRS_MID = 2048
DIRS_COARSE = 8192
FINE_BOXES = 4096
MID_BOXES = 1024
COARSE_BOXES = 256


def offset_table():
    return jnp.array(list(range(-MAX_OFFSET, -1)) + list(range(2, MAX_OFFSET + 1)), dtype=jnp.int32)


def draw_list_rows(base_key, box_count):
    region_key = jax.random.fold_in(base_key, 11)
    occupy_key = jax.random.fold_in(base_key, 12)
    shuffle_key = jax.random.fold_in(base_key, 13)
    centre = jnp.arange(box_count, dtype=jnp.int32)[:, None]
    target = centre + offset_table()[None, :]
    inside = (target >= 0) & (target < box_count) & (jnp.abs(target // 4 - centre // 4) <= 1)
    region_count = (box_count + 15) // 16
    density = jax.random.randint(region_key, (region_count,), 1, 5, dtype=jnp.int32)
    levels = jax.random.randint(occupy_key, (box_count,), 0, 4, dtype=jnp.int32)
    occupied = levels < jnp.repeat(density, 16)[:box_count]
    clipped = jnp.clip(target, 0, box_count - 1)
    present = inside & occupied[clipped] & occupied[centre]
    listed = jnp.where(present, target, -1)
    scores = jax.random.randint(shuffle_key, listed.shape, 0, 1 << 20, dtype=jnp.int32) * LIST_SLOTS + jnp.arange(LIST_SLOTS, dtype=jnp.int32)[None, :]
    slot_order = jnp.argsort(scores, axis=1, stable=True)
    return jnp.take_along_axis(listed, slot_order, axis=1).astype(jnp.int32)


def draw_child_slots(base_key, box_count):
    scores = jax.random.randint(base_key, (box_count // 4, 4), 0, 1 << 20, dtype=jnp.int32) * 4 + jnp.arange(4, dtype=jnp.int32)[None, :]
    return jnp.argsort(scores, axis=1, stable=True).reshape(box_count).astype(jnp.int32)


def draw_fine_list(key, part):
    return draw_list_rows(jax.random.fold_in(key, 1), FINE_BOXES)


def draw_middle_list(key, part):
    return draw_list_rows(jax.random.fold_in(key, 2), MID_BOXES)


def draw_coarse_list(key, part):
    return draw_list_rows(jax.random.fold_in(key, 3), COARSE_BOXES)


def draw_fine_slot(key, part):
    return draw_child_slots(jax.random.fold_in(key, 4), FINE_BOXES)


def draw_middle_slot(key, part):
    return draw_child_slots(jax.random.fold_in(key, 5), MID_BOXES)


def shard_levels(rng, extent, pieces, smallest, top_value):
    factor_of = 1.0
    for dim, blocks in pieces:
        heights = jax.random.uniform(jax.random.fold_in(jax.random.fold_in(rng, 6), dim), (blocks,), jnp.float32, smallest / len(pieces), top_value / len(pieces))
        factor_of = factor_of * jnp.repeat(jnp.exp(heights), extent[dim] // blocks).reshape((-1,) + (1,) * (len(extent) - 1 - dim))
    return factor_of


def scatter_about(stream_key, shape, scale, most, shards=(), kind=jnp.bfloat16):
    drawn = scale * jax.random.normal(stream_key, shape, jnp.float32)
    if shards:
        drawn = drawn * shard_levels(stream_key, shape, shards, -0.22, 0.18)
    return jnp.clip(drawn, -most, most).astype(kind)


def setup_inputs(seed: int = 0) -> dict:
    key_list = jax.random.split(jax.random.key(seed), 16)
    return {
        "fine_out": scatter_about(key_list[0], (FINE_BOXES, COMPONENTS, DIRS_FINE), 1.0, 6.0, ((0, 256),)),
        "fine_list": draw_fine_list(jax.random.fold_in(key_list[15], 71), 0),
        "fine_slot": draw_fine_slot(jax.random.fold_in(key_list[15], 71), 0),
        "fine_translator": scatter_about(key_list[3], (LIST_SLOTS, 2, DIRS_FINE), 0.3, 4.0, (), jnp.float32),
        "theta_up_fine": scatter_about(key_list[4], (THETA_MID, THETA_FINE), THETA_FINE ** -0.5, 1.5),
        "phi_up_fine": scatter_about(key_list[5], (PHI_MID, PHI_FINE), PHI_FINE ** -0.5, 1.0),
        "middle_phase": jnp.clip(jax.random.uniform(key_list[6], (4, DIRS_MID), jnp.float32, -3.140625, 3.140625), -3.140625, 3.140625),
        "middle_list": draw_middle_list(jax.random.fold_in(key_list[15], 71), 0),
        "middle_slot": draw_middle_slot(jax.random.fold_in(key_list[15], 71), 0),
        "middle_translator": scatter_about(key_list[9], (LIST_SLOTS, 2, DIRS_MID), 0.15, 2.0, ((2, 16),), jnp.float32),
        "theta_up_middle": scatter_about(key_list[10], (THETA_COARSE, THETA_MID), THETA_MID ** -0.5, 1.0),
        "phi_up_middle": scatter_about(key_list[11], (PHI_COARSE, PHI_MID), PHI_MID ** -0.5, 0.75),
        "coarse_phase": jnp.clip(jax.random.uniform(key_list[12], (4, DIRS_COARSE), jnp.float32, -3.140625, 3.140625), -3.140625, 3.140625),
        "coarse_list": draw_coarse_list(jax.random.fold_in(key_list[15], 71), 0),
        "coarse_translator": scatter_about(key_list[14], (LIST_SLOTS, 2, DIRS_COARSE), 0.08, 1.25, ((2, 256),), jnp.float32),
    }


def complex_times(real_part, imag_part, pattern):
    half_size = pattern.shape[-2] // 2
    pattern_real = pattern[..., :half_size, :]
    pattern_imag = pattern[..., half_size:, :]
    return jnp.concatenate([real_part * pattern_real - imag_part * pattern_imag, real_part * pattern_imag + imag_part * pattern_real], axis=-2)


def offsets_used():
    return list(range(-MAX_OFFSET, -1)) + list(range(2, MAX_OFFSET + 1))


def translate_rows(padded, entries, first_box, translator):
    row_count = entries.shape[0]
    box_ids = first_box + jnp.arange(row_count, dtype=jnp.int32)
    summed = jnp.zeros((row_count,) + padded.shape[1:], jnp.float32)
    for slot_index, offset in enumerate(offsets_used()):
        present = jnp.any(entries == (box_ids + offset)[:, None], axis=1).astype(jnp.float32)
        source = padded[MAX_OFFSET + offset:MAX_OFFSET + offset + row_count].astype(jnp.float32)
        contrib = complex_times(translator[slot_index, 0], translator[slot_index, 1], source)
        summed = summed + present[:, None, None] * contrib
    return summed


def interpolate(pattern, theta_matrix, phi_matrix):
    box_count, part_count = pattern.shape[0], pattern.shape[1]
    sample_grid = pattern.reshape(box_count * part_count, theta_matrix.shape[1], phi_matrix.shape[1]).astype(jnp.float32)
    along_phi = jnp.einsum("nap,qp->naq", sample_grid, phi_matrix.astype(jnp.float32), precision=lax.Precision.HIGHEST)
    along_phi = lax.optimization_barrier(along_phi.astype(jnp.bfloat16)).astype(jnp.float32)
    lifted = jnp.einsum("naq,ta->ntq", along_phi, theta_matrix.astype(jnp.float32), precision=lax.Precision.HIGHEST)
    return lifted.reshape(box_count, part_count, -1)


def phase_shift(values, slot_ids, angles):
    choose = (slot_ids[:, None] == jnp.arange(4, dtype=jnp.int32)[None, :]).astype(jnp.float32)
    cosine = jnp.dot(choose, jnp.cos(angles), precision=lax.Precision.HIGHEST)
    sine_part = jnp.dot(choose, jnp.sin(angles), precision=lax.Precision.HIGHEST)
    return complex_times(cosine[:, None, :], sine_part[:, None, :], values)


def sum_children(values):
    return values.reshape(values.shape[0] // 4, 4, values.shape[1], values.shape[2]).sum(axis=1)


def reference(fine_out, fine_list, fine_slot, fine_translator, theta_up_fine, phi_up_fine, middle_phase, middle_list, middle_slot, middle_translator, theta_up_middle, phi_up_middle, coarse_phase, coarse_list, coarse_translator):
    fine_pad = jnp.pad(fine_out, ((MAX_OFFSET, MAX_OFFSET), (0, 0), (0, 0)))
    fine_in = translate_rows(fine_pad, fine_list, 0, fine_translator).astype(jnp.bfloat16)

    def climb_tree(inputs):
        children, child_slots, parent_slots = inputs
        lifted = interpolate(children, theta_up_fine, phi_up_fine)
        parents = sum_children(phase_shift(lifted, child_slots, middle_phase)).astype(jnp.bfloat16)
        raised = interpolate(parents, theta_up_middle, phi_up_middle)
        coarse = sum_children(phase_shift(raised, parent_slots, coarse_phase)).astype(jnp.bfloat16)
        return parents, coarse

    middle_blocks, coarse_blocks = lax.map(climb_tree, (fine_out.reshape(COARSE_BOXES, 16, COMPONENTS, DIRS_FINE), fine_slot.reshape(COARSE_BOXES, 16), middle_slot.reshape(COARSE_BOXES, 4)))
    middle_out = middle_blocks.reshape(MID_BOXES, COMPONENTS, DIRS_MID)
    coarse_out = coarse_blocks.reshape(COARSE_BOXES, COMPONENTS, DIRS_COARSE)
    middle_pad = jnp.pad(middle_out, ((MAX_OFFSET, MAX_OFFSET), (0, 0), (0, 0)))
    middle_in = translate_rows(middle_pad, middle_list, 0, middle_translator).astype(jnp.bfloat16)
    coarse_pad = jnp.pad(coarse_out, ((MAX_OFFSET, MAX_OFFSET), (0, 0), (0, 0)))
    coarse_in = translate_rows(coarse_pad, coarse_list, 0, coarse_translator).astype(jnp.bfloat16)
    return (fine_in, middle_in, coarse_in)
```

```python
import functools

import jax
import jax.numpy as jnp
from jax import lax
from jax.experimental import pallas as pl
from jax.experimental.pallas import tpu as pltpu
from jax.sharding import PartitionSpec as P

REACH = 7
HALO = 4
ALL = ("box", "dir")
F32 = jnp.float32
BF16 = jnp.bfloat16
OFFSETS = list(range(-REACH, -1)) + list(range(2, REACH + 1))
VMEM = pl.BlockSpec(memory_space=pltpu.VMEM)
SMEM = pl.BlockSpec(memory_space=pltpu.SMEM)


def cos_sin(x):
    y = 0.5 * x
    z = y * y
    s = y * (
        1.0
        + z * (-1 / 6 + z * (1 / 120 + z * (-1 / 5040 + z * (1 / 362880 + z * (-1 / 39916800)))))
    )
    c = 1.0 + z * (
        -0.5
        + z * (1 / 24 + z * (-1 / 720 + z * (1 / 40320 + z * (-1 / 3628800 + z * (1 / 479001600)))))
    )
    return 1.0 - 2.0 * s * s, 2.0 * s * c


def iota(shape, dim):
    return lax.broadcasted_iota(jnp.int32, shape, dim)


def dot(a, b):
    return jnp.dot(a, b, preferred_element_type=F32)


def dot_nt(a, b):
    return lax.dot_general(a, b, (((1,), (1,)), ((), ())), preferred_element_type=F32)


def one_hot(cond):
    return cond.astype(F32).astype(BF16)


def phase_rows(phase_ref, slot_ref, first, count):
    row = iota((count, 128), 0)
    slot = jnp.zeros((count, 128), jnp.int32)
    for b in range(count):
        slot = jnp.where(row == b, slot_ref[first + b], slot)
    blocks = []
    for k in range(phase_ref.shape[1] // 128):
        part = phase_ref[:, k * 128 : (k + 1) * 128]
        rows = jnp.broadcast_to(part[3:4, :], (count, 128))
        for j in range(3):
            rows = jnp.where(slot == j, part[j : j + 1, :], rows)
        blocks.append(rows)
    return blocks


def fill_cos_sin(cs_ref, phase_ref, slot_ref, first):
    blocks = phase_rows(phase_ref, slot_ref, first, cs_ref.shape[1])
    for k, rows in enumerate(blocks):
        cos, sin = cos_sin(rows)
        cs_ref[0, :, k * 128 : (k + 1) * 128] = cos
        cs_ref[1, :, k * 128 : (k + 1) * 128] = sin


def middle_kernel(x_ref, theta_ref, phi_ref, phase_ref, slot_ref, out_ref, m_ref, cs_ref, l_ref):
    boxes, parts, dirs = x_ref.shape
    t_n, t2_n = theta_ref.shape
    p_n, q_n = phi_ref.shape
    wide = t2_n * q_n
    fill_cos_sin(cs_ref, phase_ref, slot_ref, lax.axis_index("dir") * boxes)
    spread = one_hot(iota((t2_n, wide), 1) // q_n == iota((t2_n, wide), 0))
    theta_row = dot(theta_ref[...], spread)
    repeat = one_hot(iota((q_n, wide), 1) % q_n == iota((q_n, wide), 0))
    phi_row = dot(phi_ref[...], repeat)
    for t in range(t_n):
        m_ref[t * p_n : (t + 1) * p_n, :] = (theta_row[t : t + 1, :] * phi_row).astype(BF16)
    x = x_ref[...].reshape(boxes * parts, dirs)
    half = parts // 2
    step = 256
    for n in range(wide // step):
        cols = slice(n * step, (n + 1) * step)
        l_ref[n % 2] = dot(x, m_ref[:, cols])
        for p in range(boxes // 4):
            re = jnp.zeros((half, step), F32)
            im = jnp.zeros((half, step), F32)
            for b in range(4 * p, 4 * p + 4):
                c = cs_ref[0, b : b + 1, cols]
                s = cs_ref[1, b : b + 1, cols]
                lr = l_ref[n % 2, b * parts : b * parts + half, :]
                li = l_ref[n % 2, b * parts + half : (b + 1) * parts, :]
                re = re + (c * lr - s * li)
                im = im + (c * li + s * lr)
            both = jnp.concatenate([re, im], axis=0).astype(BF16)
            for h in range(step // 128):
                out_ref[n * (step // 128) + h, p] = both[:, h * 128 : (h + 1) * 128]


def coarse_kernel(par_ref, theta_ref, phi_ref, phase_ref, slot_ref, out_ref, a_ref, cs_ref, l_ref):
    blocks, kids, parts, lanes = par_ref.shape
    t_n, t2_n = theta_ref.shape
    p_n, q_n = phi_ref.shape
    fill_cos_sin(cs_ref, phase_ref, slot_ref, lax.axis_index("dir") * kids)
    pair = lanes // p_n
    tall = one_hot(iota((lanes, p_n), 0) % p_n == iota((lanes, p_n), 1))
    phi_tall = dot(tall, phi_ref[...])
    w = jnp.concatenate(
        [jnp.where(iota((lanes, q_n), 0) // p_n == h, phi_tall, 0.0) for h in range(pair)], axis=1
    ).astype(BF16)
    e1 = one_hot(iota((t2_n * 8, t2_n), 0) // 8 == iota((t2_n * 8, t2_n), 1))
    e2 = one_hot(iota((t_n, t_n * 8), 1) // 8 == iota((t_n, t_n * 8), 0))
    stretched = dot(dot_nt(e1, theta_ref[...]).astype(BF16), e2)
    same = iota(stretched.shape, 0) % 8 == iota(stretched.shape, 1) % 8
    k8 = jnp.where(same, stretched, 0.0).astype(BF16)
    rows = kids * parts
    a_ref[...] = dot(par_ref[...].reshape(blocks * rows, lanes), w).reshape(blocks, rows, pair * q_n)
    for m in range(kids):
        for a in range(2):
            cols = []
            for r in (m * parts + 8 * a, m * parts + 16 + 8 * a):
                pieces = [
                    a_ref[t // pair, r : r + 8, (t % pair) * q_n : (t % pair + 1) * q_n]
                    for t in range(t_n)
                ]
                cols.append(jnp.concatenate(pieces, axis=0).astype(BF16))
            l_ref[m, a] = dot(k8, jnp.concatenate(cols, axis=1))
    lane = iota((8, q_n), 1)
    low = lane < 64
    even = lane % 64 < 32
    for t2 in range(t2_n):
        lanes_of = slice(t2 * q_n, (t2 + 1) * q_n)
        v = {}
        c = [cs_ref[0, m : m + 1, lanes_of] for m in range(kids)]
        s = [cs_ref[1, m : m + 1, lanes_of] for m in range(kids)]
        for a in range(2):
            re = jnp.zeros((8, q_n), F32)
            im = jnp.zeros((8, q_n), F32)
            for m in range(kids):
                lr = l_ref[m, a, t2 * 8 : t2 * 8 + 8, :q_n]
                li = l_ref[m, a, t2 * 8 : t2 * 8 + 8, q_n:]
                re = re + (c[m] * lr - s[m] * li)
                im = im + (c[m] * li + s[m] * lr)
            v[0, a] = re
            v[1, a] = im
        u = {}
        for a in range(2):
            u[0, a] = jnp.where(low, v[0, a], pltpu.roll(v[1, a], 64, 1))
            u[1, a] = jnp.where(low, pltpu.roll(v[0, a], 64, 1), v[1, a])
        for h in range(2):
            out_ref[t2 * 4 + 2 * h] = jnp.where(even, u[h, 0], pltpu.roll(u[h, 1], 32, 1)).astype(BF16)
            out_ref[t2 * 4 + 2 * h + 1] = jnp.where(
                even, pltpu.roll(u[h, 0], 96, 1), u[h, 1]
            ).astype(BF16)


def codes_by_lane(list_ref, first):
    entry = list_ref[...]
    place = entry - (first + iota(entry.shape, 1)) + REACH
    bits = jnp.where(entry >= 0, lax.shift_left(jnp.ones_like(entry), jnp.maximum(place, 0)), 0)
    row = jnp.sum(bits.astype(F32), axis=0, keepdims=True)
    return jnp.transpose(jnp.broadcast_to(row, (8, row.shape[1])))[:, :1].astype(jnp.int32)


def codes_by_row(list_ref, first):
    entry = list_ref[...]
    place = entry - (first + iota(entry.shape, 0)) + REACH
    bits = jnp.where(entry >= 0, lax.shift_left(jnp.ones_like(entry), jnp.maximum(place, 0)), 0)
    return jnp.sum(bits.astype(F32), axis=1, keepdims=True).astype(jnp.int32)


def masked(code, offset):
    return lax.bitwise_and(code, 1 << (offset + REACH)) != 0


def group_offsets(r):
    return [o for o in OFFSETS if -HALO <= r + o < 2 * HALO]


def translate_kernel(axes, by_row, x_ref, lo_ref, hi_ref, list_ref, tr_ref, out_ref, f_ref, mt_ref):
    boxes, parts, dirs = x_ref.shape
    half = parts // 2
    first = lax.axis_index(axes[0])
    for name in axes[1:]:
        first = first * lax.axis_size(name) + lax.axis_index(name)
    first = first * boxes
    code = (codes_by_row if by_row else codes_by_lane)(list_ref, first)
    code = jnp.broadcast_to(code, (boxes, 128))
    for k in range(dirs // 128):
        cols = slice(k * 128, (k + 1) * 128)
        for slot, o in enumerate(OFFSETS):
            here = masked(code, o)
            mt_ref[slot, 0, :, cols] = jnp.where(here, tr_ref[slot, 0:1, cols], 0.0)
            mt_ref[slot, 1, :, cols] = jnp.where(here, tr_ref[slot, 1:2, cols], 0.0)
    f_ref[:HALO] = lo_ref[...].astype(F32)
    f_ref[HALO : HALO + boxes] = x_ref[...].astype(F32)
    f_ref[HALO + boxes :] = hi_ref[...].astype(F32)

    def group(g, cols):
        for r in range(4):
            i = 4 * g + r
            re = jnp.zeros((half, 128), F32)
            im = jnp.zeros((half, 128), F32)
            for o in group_offsets(r):
                slot = OFFSETS.index(o)
                a = mt_ref[slot, 0, i : i + 1, cols]
                b = mt_ref[slot, 1, i : i + 1, cols]
                xr = f_ref[i + HALO + o, :half, cols]
                xi = f_ref[i + HALO + o, half:, cols]
                re = re + (a * xr - b * xi)
                im = im + (a * xi + b * xr)
            out_ref[i, :, cols] = jnp.concatenate([re, im], axis=0).astype(BF16)

    for k in range(dirs // 128):
        cols = slice(k * 128, (k + 1) * 128)

        for g in range(boxes // 4):
            group(g, cols)


def coarse_masks_kernel(list_ref, tr_ref, out_ref):
    boxes = out_ref.shape[2]
    code = jnp.broadcast_to(codes_by_lane(list_ref, 0), (boxes, 128))
    low = iota((1, 128), 1) < 64
    for slot, o in enumerate(OFFSETS):
        here = masked(code, o)
        a = jnp.concatenate([tr_ref[slot, 0:1, :]] * 4, axis=1)
        b = jnp.concatenate([tr_ref[slot, 1:2, :]] * 4, axis=1)
        b = jnp.where(low, -b, b)
        out_ref[slot, 0] = jnp.where(here, a, 0.0)
        out_ref[slot, 1] = jnp.where(here, b, 0.0)


def coarse_translate_kernel(x_ref, mt_ref, out_ref, f_ref, r_ref, y_ref):
    boxes, sub, lanes = x_ref.shape
    zero = jnp.zeros((HALO, sub, lanes), F32)
    for ref in (f_ref, r_ref):
        ref[:HALO] = zero
        ref[HALO + boxes :] = zero
    x = x_ref[...].astype(F32)
    f_ref[HALO : HALO + boxes] = x
    r_ref[HALO : HALO + boxes] = pltpu.roll(x.reshape(boxes * sub, lanes), 64, 1).reshape(x.shape)

    for g in range(boxes // 4):
        for r in range(4):
            i = 4 * g + r
            acc = jnp.zeros((sub, lanes), F32)
            for o in group_offsets(r):
                slot = OFFSETS.index(o)
                a = mt_ref[slot, 0, i : i + 1, :]
                b = mt_ref[slot, 1, i : i + 1, :]
                acc = acc + (a * f_ref[i + HALO + o] + b * r_ref[i + HALO + o])
            y_ref[i * sub : (i + 1) * sub, :] = acc
    for s in range(sub):
        turned = jnp.transpose(y_ref[pl.ds(s, boxes, stride=sub), :])
        for cb in range(4):
            out_ref[8 * cb + s] = turned[32 * cb : 32 * cb + 32, :].astype(BF16)


def call(body, out, specs, scratch, *args):
    return pl.pallas_call(
        body,
        out_shape=out,
        in_specs=specs,
        out_specs=VMEM,
        scratch_shapes=scratch,
    )(*args)


def halo(x, axes):
    count = lax.axis_size(axes)
    up = [(i, i + 1) for i in range(count - 1)]
    down = [(i + 1, i) for i in range(count - 1)]
    return lax.ppermute(x[-HALO:], axes, up), lax.ppermute(x[:HALO], axes, down)


def local(
    fine_out,
    fine_list,
    fine_slot,
    fine_translator,
    theta_up_fine,
    phi_up_fine,
    middle_phase,
    middle_list,
    middle_slot,
    middle_translator,
    theta_up_middle,
    phi_up_middle,
    coarse_phase,
    coarse_list,
    coarse_translator,
):
    shape = jax.ShapeDtypeStruct
    boxes, parts, dirs = fine_out.shape
    dir_n = lax.axis_size("dir")
    all_n = dir_n * lax.axis_size("box")
    wide = middle_phase.shape[1]
    widest = coarse_phase.shape[1]
    kids = boxes // 4
    parents = call(
        middle_kernel,
        shape((dir_n, kids, parts, wide // dir_n), BF16),
        [VMEM] * 4 + [SMEM],
        [
            pltpu.VMEM((dirs, wide), BF16),
            pltpu.VMEM((2, boxes, wide), F32),
            pltpu.VMEM((2, boxes * parts, 256), F32),
        ],
        fine_out,
        theta_up_fine.T,
        phi_up_fine.T,
        middle_phase,
        fine_slot,
    )
    t2_n = theta_up_middle.shape[0]
    q_n = phi_up_middle.shape[0]
    chunks = call(
        coarse_kernel,
        shape((all_n, 8, 128), BF16),
        [VMEM] * 4 + [SMEM],
        [
            pltpu.VMEM((dir_n, kids * parts, 2 * q_n), F32),
            pltpu.VMEM((2, kids, widest), F32),
            pltpu.VMEM((kids, 2, t2_n * 8, 2 * q_n), F32),
        ],
        parents,
        theta_up_middle.T,
        phi_up_middle.T,
        coarse_phase,
        middle_slot,
    )
    coarse_held = lax.all_to_all(chunks, ALL, split_axis=0, concat_axis=0, tiled=True)
    parents, fine_late, chunks = lax.optimization_barrier((parents, fine_out, chunks))
    middle_out = lax.all_to_all(parents, "dir", split_axis=0, concat_axis=0, tiled=True)
    middle_out = middle_out.reshape(dir_n * kids, parts, -1)
    fine_lo, fine_hi = halo(fine_late, ALL)
    fine_in = call(
        functools.partial(translate_kernel, ALL, True),
        shape(fine_out.shape, BF16),
        [VMEM] * 5,
        [
            pltpu.VMEM((boxes + 2 * HALO, parts, dirs), F32),
            pltpu.VMEM((12, 2, boxes, dirs), F32),
        ],
        fine_out,
        fine_lo,
        fine_hi,
        fine_list,
        fine_translator,
    )
    masks = call(
        coarse_masks_kernel,
        shape((12, 2, all_n, 128), F32),
        [VMEM] * 2,
        [],
        coarse_list.T,
        coarse_translator,
    )
    middle_lo, middle_hi = halo(middle_out, "box")
    held, _, lanes = middle_out.shape
    middle_in = call(
        functools.partial(translate_kernel, ("box",), False),
        shape(middle_out.shape, BF16),
        [VMEM] * 5,
        [
            pltpu.VMEM((held + 2 * HALO, parts, lanes), F32),
            pltpu.VMEM((12, 2, held, lanes), F32),
        ],
        middle_out,
        middle_lo,
        middle_hi,
        middle_list.T,
        middle_translator,
    )
    coarse_in = call(
        coarse_translate_kernel,
        shape((parts, widest // all_n, all_n), BF16),
        [VMEM] * 2,
        [
            pltpu.VMEM((all_n + 2 * HALO, 8, 128), F32),
            pltpu.VMEM((all_n + 2 * HALO, 8, 128), F32),
            pltpu.VMEM((all_n * 8, 128), F32),
        ],
        coarse_held,
        masks,
    )
    return fine_in, middle_in, jnp.transpose(coarse_in, (2, 0, 1))


def solution(mesh):
    return jax.shard_map(
        local,
        mesh=mesh,
        in_specs=(
            P(ALL, None, None),
            P(ALL, None),
            P("box"),
            P(),
            P(),
            P(),
            P(),
            P("box", None),
            P("box"),
            P(None, None, "dir"),
            P(),
            P(),
            P(),
            P(),
            P(None, None, ALL),
        ),
        out_specs=(P(ALL, None, None), P("box", None, "dir"), P(None, None, ALL)),
        check_vma=False,
    )
```

```python
import functools

import jax
import jax.numpy as jnp
from jax import lax
from jax.experimental import pallas as pl
from jax.experimental.pallas import tpu as pltpu
from jax.sharding import PartitionSpec as P


REACH = 7
HALO = 4
ALL = ("box", "dir")
F32 = jnp.float32
BF16 = jnp.bfloat16
OFFSETS = list(range(-REACH, -1)) + list(range(2, REACH + 1))
VMEM = pl.BlockSpec(memory_space=pltpu.VMEM)
SMEM = pl.BlockSpec(memory_space=pltpu.SMEM)


def cos_sin(x):
    y = 0.5 * x
    z = y * y
    s = y * (
        1.0
        + z * (-1 / 6 + z * (1 / 120 + z * (-1 / 5040 + z * (1 / 362880 + z * (-1 / 39916800)))))
    )
    c = 1.0 + z * (
        -0.5
        + z * (1 / 24 + z * (-1 / 720 + z * (1 / 40320 + z * (-1 / 3628800 + z * (1 / 479001600)))))
    )
    return 1.0 - 2.0 * s * s, 2.0 * s * c


def iota(shape, dim):
    return lax.broadcasted_iota(jnp.int32, shape, dim)


def dot(a, b):
    return jnp.dot(a, b, preferred_element_type=F32)


def dot_nt(a, b):
    return lax.dot_general(a, b, (((1,), (1,)), ((), ())), preferred_element_type=F32)


def one_hot(cond):
    return cond.astype(F32).astype(BF16)


def phase_rows(phase_ref, slot_ref, first, count):
    row = iota((count, 128), 0)
    slot = jnp.zeros((count, 128), jnp.int32)
    for b in range(count):
        slot = jnp.where(row == b, slot_ref[first + b], slot)
    blocks = []
    for k in range(phase_ref.shape[1] // 128):
        part = phase_ref[:, k * 128 : (k + 1) * 128]
        rows = jnp.broadcast_to(part[3:4, :], (count, 128))
        for j in range(3):
            rows = jnp.where(slot == j, part[j : j + 1, :], rows)
        blocks.append(rows)
    return blocks


def fill_cos_sin(cs_ref, phase_ref, slot_ref, first):
    blocks = phase_rows(phase_ref, slot_ref, first, cs_ref.shape[1])
    for k, rows in enumerate(blocks):
        cos, sin = cos_sin(rows)
        cs_ref[0, :, k * 128 : (k + 1) * 128] = cos
        cs_ref[1, :, k * 128 : (k + 1) * 128] = sin


def middle_kernel(x_ref, theta_ref, phi_ref, phase_ref, slot_ref, out_ref, m_ref, cs_ref, l_ref):
    boxes, parts, dirs = x_ref.shape
    t_n, t2_n = theta_ref.shape
    p_n, q_n = phi_ref.shape
    wide = t2_n * q_n
    fill_cos_sin(cs_ref, phase_ref, slot_ref, lax.axis_index("dir") * boxes)
    spread = one_hot(iota((t2_n, wide), 1) // q_n == iota((t2_n, wide), 0))
    theta_row = dot(theta_ref[...], spread)
    repeat = one_hot(iota((q_n, wide), 1) % q_n == iota((q_n, wide), 0))
    phi_row = dot(phi_ref[...], repeat)
    for t in range(t_n):
        m_ref[t * p_n : (t + 1) * p_n, :] = (theta_row[t : t + 1, :] * phi_row).astype(BF16)
    x = x_ref[...].reshape(boxes * parts, dirs)
    half = parts // 2
    step = 256
    for n in range(wide // step):
        cols = slice(n * step, (n + 1) * step)
        l_ref[n % 2] = dot(x, m_ref[:, cols])
        for p in range(boxes // 4):
            re = jnp.zeros((half, step), F32)
            im = jnp.zeros((half, step), F32)
            for b in range(4 * p, 4 * p + 4):
                c = cs_ref[0, b : b + 1, cols]
                s = cs_ref[1, b : b + 1, cols]
                lr = l_ref[n % 2, b * parts : b * parts + half, :]
                li = l_ref[n % 2, b * parts + half : (b + 1) * parts, :]
                re = re + (c * lr - s * li)
                im = im + (c * li + s * lr)
            both = jnp.concatenate([re, im], axis=0).astype(BF16)
            for h in range(step // 128):
                out_ref[n * (step // 128) + h, p] = both[:, h * 128 : (h + 1) * 128]


def coarse_kernel(par_ref, theta_ref, phi_ref, phase_ref, slot_ref, out_ref, a_ref, cs_ref, l_ref):
    blocks, kids, parts, lanes = par_ref.shape
    t_n, t2_n = theta_ref.shape
    p_n, q_n = phi_ref.shape
    fill_cos_sin(cs_ref, phase_ref, slot_ref, lax.axis_index("dir") * kids)
    pair = lanes // p_n
    tall = one_hot(iota((lanes, p_n), 0) % p_n == iota((lanes, p_n), 1))
    phi_tall = dot(tall, phi_ref[...])
    w = jnp.concatenate(
        [jnp.where(iota((lanes, q_n), 0) // p_n == h, phi_tall, 0.0) for h in range(pair)], axis=1
    ).astype(BF16)
    e1 = one_hot(iota((t2_n * 8, t2_n), 0) // 8 == iota((t2_n * 8, t2_n), 1))
    e2 = one_hot(iota((t_n, t_n * 8), 1) // 8 == iota((t_n, t_n * 8), 0))
    stretched = dot(dot_nt(e1, theta_ref[...]).astype(BF16), e2)
    same = iota(stretched.shape, 0) % 8 == iota(stretched.shape, 1) % 8
    k8 = jnp.where(same, stretched, 0.0).astype(BF16)
    rows = kids * parts
    a_ref[...] = dot(par_ref[...].reshape(blocks * rows, lanes), w).reshape(blocks, rows, pair * q_n)
    for m in range(kids):
        for a in range(2):
            cols = []
            for r in (m * parts + 8 * a, m * parts + 16 + 8 * a):
                pieces = [
                    a_ref[t // pair, r : r + 8, (t % pair) * q_n : (t % pair + 1) * q_n]
                    for t in range(t_n)
                ]
                cols.append(jnp.concatenate(pieces, axis=0).astype(BF16))
            l_ref[m, a] = dot(k8, jnp.concatenate(cols, axis=1))
    lane = iota((8, q_n), 1)
    low = lane < 64
    even = lane % 64 < 32
    for t2 in range(t2_n):
        lanes_of = slice(t2 * q_n, (t2 + 1) * q_n)
        v = {}
        c = [cs_ref[0, m : m + 1, lanes_of] for m in range(kids)]
        s = [cs_ref[1, m : m + 1, lanes_of] for m in range(kids)]
        for a in range(2):
            re = jnp.zeros((8, q_n), F32)
            im = jnp.zeros((8, q_n), F32)
            for m in range(kids):
                lr = l_ref[m, a, t2 * 8 : t2 * 8 + 8, :q_n]
                li = l_ref[m, a, t2 * 8 : t2 * 8 + 8, q_n:]
                re = re + (c[m] * lr - s[m] * li)
                im = im + (c[m] * li + s[m] * lr)
            v[0, a] = re
            v[1, a] = im
        u = {}
        for a in range(2):
            u[0, a] = jnp.where(low, v[0, a], pltpu.roll(v[1, a], 64, 1))
            u[1, a] = jnp.where(low, pltpu.roll(v[0, a], 64, 1), v[1, a])
        for h in range(2):
            out_ref[t2 * 4 + 2 * h] = jnp.where(even, u[h, 0], pltpu.roll(u[h, 1], 32, 1)).astype(BF16)
            out_ref[t2 * 4 + 2 * h + 1] = jnp.where(
                even, pltpu.roll(u[h, 0], 96, 1), u[h, 1]
            ).astype(BF16)


def codes_by_lane(list_ref, first):
    entry = list_ref[...]
    place = entry - (first + iota(entry.shape, 1)) + REACH
    bits = jnp.where(entry >= 0, lax.shift_left(jnp.ones_like(entry), jnp.maximum(place, 0)), 0)
    row = jnp.sum(bits.astype(F32), axis=0, keepdims=True)
    return jnp.transpose(jnp.broadcast_to(row, (8, row.shape[1])))[:, :1].astype(jnp.int32)


def codes_by_row(list_ref, first):
    entry = list_ref[...]
    place = entry - (first + iota(entry.shape, 0)) + REACH
    bits = jnp.where(entry >= 0, lax.shift_left(jnp.ones_like(entry), jnp.maximum(place, 0)), 0)
    return jnp.sum(bits.astype(F32), axis=1, keepdims=True).astype(jnp.int32)


def masked(code, offset):
    return lax.bitwise_and(code, 1 << (offset + REACH)) != 0


def group_offsets(r):
    return [o for o in OFFSETS if -HALO <= r + o < 2 * HALO]


def translate_kernel(axes, by_row, x_ref, lo_ref, hi_ref, list_ref, tr_ref, out_ref, f_ref, mt_ref):
    boxes, parts, dirs = x_ref.shape
    half = parts // 2
    first = lax.axis_index(axes[0])
    for name in axes[1:]:
        first = first * lax.axis_size(name) + lax.axis_index(name)
    first = first * boxes
    code = (codes_by_row if by_row else codes_by_lane)(list_ref, first)
    code = jnp.broadcast_to(code, (boxes, 128))
    for k in range(dirs // 128):
        cols = slice(k * 128, (k + 1) * 128)
        for slot, o in enumerate(OFFSETS):
            here = masked(code, o)
            mt_ref[slot, 0, :, cols] = jnp.where(here, tr_ref[slot, 0:1, cols], 0.0)
            mt_ref[slot, 1, :, cols] = jnp.where(here, tr_ref[slot, 1:2, cols], 0.0)
    f_ref[:HALO] = lo_ref[...].astype(F32)
    f_ref[HALO : HALO + boxes] = x_ref[...].astype(F32)
    f_ref[HALO + boxes :] = hi_ref[...].astype(F32)

    def group(g, cols):
        for r in range(4):
            i = 4 * g + r
            re = jnp.zeros((half, 128), F32)
            im = jnp.zeros((half, 128), F32)
            for o in group_offsets(r):
                slot = OFFSETS.index(o)
                a = mt_ref[slot, 0, i : i + 1, cols]
                b = mt_ref[slot, 1, i : i + 1, cols]
                xr = f_ref[i + HALO + o, :half, cols]
                xi = f_ref[i + HALO + o, half:, cols]
                re = re + (a * xr - b * xi)
                im = im + (a * xi + b * xr)
            out_ref[i, :, cols] = jnp.concatenate([re, im], axis=0).astype(BF16)

    for k in range(dirs // 128):
        cols = slice(k * 128, (k + 1) * 128)

        for g in range(boxes // 4):
            group(g, cols)


def coarse_masks_kernel(list_ref, tr_ref, out_ref):
    boxes = out_ref.shape[2]
    code = jnp.broadcast_to(codes_by_lane(list_ref, 0), (boxes, 128))
    low = iota((1, 128), 1) < 64
    for slot, o in enumerate(OFFSETS):
        here = masked(code, o)
        a = jnp.concatenate([tr_ref[slot, 0:1, :]] * 4, axis=1)
        b = jnp.concatenate([tr_ref[slot, 1:2, :]] * 4, axis=1)
        b = jnp.where(low, -b, b)
        out_ref[slot, 0] = jnp.where(here, a, 0.0)
        out_ref[slot, 1] = jnp.where(here, b, 0.0)


def coarse_translate_kernel(x_ref, mt_ref, out_ref, f_ref, r_ref, y_ref):
    boxes, sub, lanes = x_ref.shape
    zero = jnp.zeros((HALO, sub, lanes), F32)
    for ref in (f_ref, r_ref):
        ref[:HALO] = zero
        ref[HALO + boxes :] = zero
    x = x_ref[...].astype(F32)
    f_ref[HALO : HALO + boxes] = x
    r_ref[HALO : HALO + boxes] = pltpu.roll(x.reshape(boxes * sub, lanes), 64, 1).reshape(x.shape)

    for g in range(boxes // 4):
        for r in range(4):
            i = 4 * g + r
            acc = jnp.zeros((sub, lanes), F32)
            for o in group_offsets(r):
                slot = OFFSETS.index(o)
                a = mt_ref[slot, 0, i : i + 1, :]
                b = mt_ref[slot, 1, i : i + 1, :]
                acc = acc + (a * f_ref[i + HALO + o] + b * r_ref[i + HALO + o])
            y_ref[i * sub : (i + 1) * sub, :] = acc
    for s in range(sub):
        turned = jnp.transpose(y_ref[pl.ds(s, boxes, stride=sub), :])
        for cb in range(4):
            out_ref[8 * cb + s] = turned[32 * cb : 32 * cb + 32, :].astype(BF16)


def near(x):
    return pltpu.with_memory_space_constraint(x, pltpu.VMEM)


def call(body, out, specs, scratch, *args, limit=24 << 20):
    return pl.pallas_call(
        body,
        out_shape=out,
        in_specs=specs,
        out_specs=VMEM,
        scratch_shapes=scratch,
        compiler_params=pltpu.CompilerParams(vmem_limit_bytes=limit),
    )(*args)


def halo(x, axes):
    count = lax.axis_size(axes)
    up = [(i, i + 1) for i in range(count - 1)]
    down = [(i + 1, i) for i in range(count - 1)]
    return lax.ppermute(x[-HALO:], axes, up), lax.ppermute(x[:HALO], axes, down)


def local(
    fine_out,
    fine_list,
    fine_slot,
    fine_translator,
    theta_up_fine,
    phi_up_fine,
    middle_phase,
    middle_list,
    middle_slot,
    middle_translator,
    theta_up_middle,
    phi_up_middle,
    coarse_phase,
    coarse_list,
    coarse_translator,
):
    shape = jax.ShapeDtypeStruct
    boxes, parts, dirs = fine_out.shape
    dir_n = lax.axis_size("dir")
    all_n = dir_n * lax.axis_size("box")
    wide = middle_phase.shape[1]
    widest = coarse_phase.shape[1]
    kids = boxes // 4
    parents = call(
        middle_kernel,
        pltpu.VMEM((dir_n, kids, parts, wide // dir_n), BF16),
        [VMEM] * 4 + [SMEM],
        [
            pltpu.VMEM((dirs, wide), BF16),
            pltpu.VMEM((2, boxes, wide), F32),
            pltpu.VMEM((2, boxes * parts, 256), F32),
        ],
        fine_out,
        theta_up_fine.T,
        phi_up_fine.T,
        middle_phase,
        fine_slot,
        limit=60 * 1024 * 1024,
    )
    t2_n = theta_up_middle.shape[0]
    q_n = phi_up_middle.shape[0]
    chunks = call(coarse_kernel,
        pltpu.VMEM((all_n, 8, 128), BF16),
        [VMEM] * 4 + [SMEM],
        [
            pltpu.VMEM((dir_n, kids * parts, 2 * q_n), F32),
            pltpu.VMEM((2, kids, widest), F32),
            pltpu.VMEM((kids, 2, t2_n * 8, 2 * q_n), F32),
        ],
        near(parents),
        theta_up_middle.T,
        phi_up_middle.T,
        coarse_phase,
        middle_slot,
        limit=60 * 1024 * 1024,
    )
    coarse_held = lax.all_to_all(chunks, ALL, split_axis=0, concat_axis=0, tiled=True)
    fine_late = fine_out
    middle_out = lax.all_to_all(parents, "dir", split_axis=0, concat_axis=0, tiled=True)
    middle_out = middle_out.reshape(dir_n * kids, parts, -1)
    fine_lo, fine_hi = halo(fine_late, ALL)
    fine_in = call(
        functools.partial(translate_kernel, ALL, True),
        shape(fine_out.shape, BF16),
        [VMEM] * 5,
        [
            pltpu.VMEM((boxes + 2 * HALO, parts, dirs), F32),
            pltpu.VMEM((12, 2, boxes, dirs), F32),
        ],
        fine_out,
        near(fine_lo),
        near(fine_hi),
        fine_list,
        fine_translator,
    )
    masks = call(
        coarse_masks_kernel,
        pltpu.VMEM((12, 2, all_n, 128), F32),
        [VMEM] * 2,
        [],
        coarse_list.T,
        coarse_translator,
    )
    middle_lo, middle_hi = halo(middle_out, "box")
    held, _, lanes = middle_out.shape
    middle_in = call(functools.partial(translate_kernel, ("box",), False),
        shape(middle_out.shape, BF16),
        [VMEM] * 5,
        [
            pltpu.VMEM((held + 2 * HALO, parts, lanes), F32),
            pltpu.VMEM((12, 2, held, lanes), F32),
        ],
        near(middle_out),
        near(middle_lo),
        near(middle_hi),
        middle_list.T,
        middle_translator,
    )
    coarse_in = call(
        coarse_translate_kernel,
        shape((parts, widest // all_n, all_n), BF16),
        [VMEM] * 2,
        [
            pltpu.VMEM((all_n + 2 * HALO, 8, 128), F32),
            pltpu.VMEM((all_n + 2 * HALO, 8, 128), F32),
            pltpu.VMEM((all_n * 8, 128), F32),
        ],
        near(coarse_held),
        near(masks),
    )
    return fine_in, middle_in, jnp.transpose(coarse_in, (2, 0, 1))


def solution(mesh):
    return jax.shard_map(
        local,
        mesh=mesh,
        in_specs=(
            P(ALL, None, None),
            P(ALL, None),
            P("box"),
            P(),
            P(),
            P(),
            P(),
            P("box", None),
            P("box"),
            P(None, None, "dir"),
            P(),
            P(),
            P(),
            P(),
            P(None, None, ALL),
        ),
        out_specs=(P(ALL, None, None), P("box", None, "dir"), P(None, None, ALL)),
        check_vma=False,
    )
```

```python
import functools

import jax
import jax.numpy as jnp
from jax import lax
from jax.experimental import pallas as pl
from jax.experimental.pallas import tpu as pltpu
from jax.sharding import PartitionSpec as P


REACH = 7
HALO = 4
ALL = ("box", "dir")
F32 = jnp.float32
BF16 = jnp.bfloat16
OFFSETS = list(range(-REACH, -1)) + list(range(2, REACH + 1))
VMEM = pl.BlockSpec(memory_space=pltpu.VMEM)
SMEM = pl.BlockSpec(memory_space=pltpu.SMEM)


def cos_sin(x):
    y = 0.5 * x
    z = y * y
    s = y * (
        1.0
        + z * (-1 / 6 + z * (1 / 120 + z * (-1 / 5040 + z * (1 / 362880 + z * (-1 / 39916800)))))
    )
    c = 1.0 + z * (
        -0.5
        + z * (1 / 24 + z * (-1 / 720 + z * (1 / 40320 + z * (-1 / 3628800 + z * (1 / 479001600)))))
    )
    return 1.0 - 2.0 * s * s, 2.0 * s * c


def iota(shape, dim):
    return lax.broadcasted_iota(jnp.int32, shape, dim)


def dot(a, b):
    return jnp.dot(a, b, preferred_element_type=F32)


def dot_nt(a, b):
    return lax.dot_general(a, b, (((1,), (1,)), ((), ())), preferred_element_type=F32)


def one_hot(cond):
    return cond.astype(F32).astype(BF16)


def phase_rows(phase_ref, slot_ref, first, count):
    row = iota((count, 128), 0)
    slot = jnp.zeros((count, 128), jnp.int32)
    for b in range(count):
        slot = jnp.where(row == b, slot_ref[first + b], slot)
    blocks = []
    for k in range(phase_ref.shape[1] // 128):
        part = phase_ref[:, k * 128 : (k + 1) * 128]
        rows = jnp.broadcast_to(part[3:4, :], (count, 128))
        for j in range(3):
            rows = jnp.where(slot == j, part[j : j + 1, :], rows)
        blocks.append(rows)
    return blocks


def fill_cos_sin(cs_ref, phase_ref, slot_ref, first):
    blocks = phase_rows(phase_ref, slot_ref, first, cs_ref.shape[1])
    for k, rows in enumerate(blocks):
        cos, sin = cos_sin(rows)
        cs_ref[0, :, k * 128 : (k + 1) * 128] = cos
        cs_ref[1, :, k * 128 : (k + 1) * 128] = sin


def middle_kernel(
    x_ref,
    theta_ref,
    phi_ref,
    phase_ref,
    slot_ref,
    out_ref,
    y0_ref,
    y1_ref,
    y2_ref,
    y3_ref,
    ea_ref,
    eb_ref,
    m_ref,
    cs_ref,
    l_ref,
):
    boxes, parts, dirs = x_ref.shape
    t_n, t2_n = theta_ref.shape
    p_n, q_n = phi_ref.shape
    wide = t2_n * q_n
    fill_cos_sin(cs_ref, phase_ref, slot_ref, lax.axis_index("dir") * boxes)
    spread = one_hot(iota((t2_n, wide), 1) // q_n == iota((t2_n, wide), 0))
    theta_row = dot(theta_ref[...], spread)
    repeat = one_hot(iota((q_n, wide), 1) % q_n == iota((q_n, wide), 0))
    phi_row = dot(phi_ref[...], repeat)
    for t in range(t_n):
        m_ref[t * p_n : (t + 1) * p_n, :] = (theta_row[t : t + 1, :] * phi_row).astype(BF16)
    mine = lax.axis_index("dir")
    core = mine % 2
    ea_ref[...] = x_ref[pl.ds((1 - core) * (boxes - HALO), HALO)]
    eb_ref[...] = x_ref[pl.ds(core * (boxes - HALO), HALO)]
    x = x_ref[...].reshape(boxes * parts, dirs)
    half = parts // 2
    step = 256
    same = jnp.broadcast_to(core, (parts, 128)) == 0
    for e in range(wide // step):
        n = lax.bitwise_xor(mine // 2, e)
        cols = pl.ds(pl.multiple_of(n * step, step), step)
        l_ref[e % 2] = dot(x, m_ref[:, cols])
        for p in range(boxes // 4):
            re = jnp.zeros((half, step), F32)
            im = jnp.zeros((half, step), F32)
            for b in range(4 * p, 4 * p + 4):
                c = cs_ref[0, b : b + 1, cols]
                s = cs_ref[1, b : b + 1, cols]
                lr = l_ref[e % 2, b * parts : b * parts + half, :]
                li = l_ref[e % 2, b * parts + half : (b + 1) * parts, :]
                re = re + (c * lr - s * li)
                im = im + (c * li + s * lr)
            both = jnp.concatenate([re, im], axis=0)
            first = both[:, :128]
            second = both[:, 128:]
            out_ref[2 * n, p] = first.astype(BF16)
            out_ref[2 * n + 1, p] = second.astype(BF16)
            to = (y0_ref, y1_ref, y2_ref, y3_ref)[e % 4]
            to[e // 4, 0, p] = jnp.where(same, first, second).astype(BF16)
            to[e // 4, 1, p] = jnp.where(same, second, first).astype(BF16)


def coarse_kernel(par_ref, theta_ref, phi_ref, phase_ref, slot_ref, out_ref, a_ref, cs_ref, l_ref):
    blocks, kids, parts, lanes = par_ref.shape
    t_n, t2_n = theta_ref.shape
    p_n, q_n = phi_ref.shape
    fill_cos_sin(cs_ref, phase_ref, slot_ref, lax.axis_index("dir") * kids)
    pair = lanes // p_n
    tall = one_hot(iota((lanes, p_n), 0) % p_n == iota((lanes, p_n), 1))
    phi_tall = dot(tall, phi_ref[...])
    w = jnp.concatenate(
        [jnp.where(iota((lanes, q_n), 0) // p_n == h, phi_tall, 0.0) for h in range(pair)], axis=1
    ).astype(BF16)
    e1 = one_hot(iota((t2_n * 8, t2_n), 0) // 8 == iota((t2_n * 8, t2_n), 1))
    e2 = one_hot(iota((t_n, t_n * 8), 1) // 8 == iota((t_n, t_n * 8), 0))
    stretched = dot(dot_nt(e1, theta_ref[...]).astype(BF16), e2)
    same = iota(stretched.shape, 0) % 8 == iota(stretched.shape, 1) % 8
    k8 = jnp.where(same, stretched, 0.0).astype(BF16)
    rows = kids * parts
    a_ref[...] = dot(par_ref[...].reshape(blocks * rows, lanes), w).reshape(blocks, rows, pair * q_n)
    for m in range(kids):
        for a in range(2):
            cols = []
            for r in (m * parts + 8 * a, m * parts + 16 + 8 * a):
                pieces = [
                    a_ref[t // pair, r : r + 8, (t % pair) * q_n : (t % pair + 1) * q_n]
                    for t in range(t_n)
                ]
                cols.append(jnp.concatenate(pieces, axis=0).astype(BF16))
            l_ref[m, a] = dot(k8, jnp.concatenate(cols, axis=1))
    lane = iota((8, q_n), 1)
    low = lane < 64
    even = lane % 64 < 32
    for t2 in range(t2_n):
        lanes_of = slice(t2 * q_n, (t2 + 1) * q_n)
        v = {}
        c = [cs_ref[0, m : m + 1, lanes_of] for m in range(kids)]
        s = [cs_ref[1, m : m + 1, lanes_of] for m in range(kids)]
        for a in range(2):
            re = jnp.zeros((8, q_n), F32)
            im = jnp.zeros((8, q_n), F32)
            for m in range(kids):
                lr = l_ref[m, a, t2 * 8 : t2 * 8 + 8, :q_n]
                li = l_ref[m, a, t2 * 8 : t2 * 8 + 8, q_n:]
                re = re + (c[m] * lr - s[m] * li)
                im = im + (c[m] * li + s[m] * lr)
            v[0, a] = re
            v[1, a] = im
        u = {}
        for a in range(2):
            u[0, a] = jnp.where(low, v[0, a], pltpu.roll(v[1, a], 64, 1))
            u[1, a] = jnp.where(low, pltpu.roll(v[0, a], 64, 1), v[1, a])
        for h in range(2):
            out_ref[t2 * 4 + 2 * h] = jnp.where(even, u[h, 0], pltpu.roll(u[h, 1], 32, 1)).astype(BF16)
            out_ref[t2 * 4 + 2 * h + 1] = jnp.where(
                even, pltpu.roll(u[h, 0], 96, 1), u[h, 1]
            ).astype(BF16)


def pack_x_kernel(y0_ref, y1_ref, y2_ref, y3_ref, out_ref):
    for y, ref in enumerate((y0_ref, y1_ref, y2_ref, y3_ref)):
        out_ref[y] = ref[1]


def pack_core_kernel(y0_ref, y1_ref, y2_ref, y3_ref, x_ref, out_ref):
    for y, ref in enumerate((y0_ref, y1_ref, y2_ref, y3_ref)):
        out_ref[0, y] = ref[0, 1]
        out_ref[1, y] = x_ref[y, 1]


def gather_kernel(y0_ref, y1_ref, y2_ref, y3_ref, x_ref, c_ref, out_ref, ea_ref, eb_ref):
    mine = lax.axis_index("dir")
    for y, ref in enumerate((y0_ref, y1_ref, y2_ref, y3_ref)):
        out_ref[lax.bitwise_xor(mine, 2 * y)] = ref[0, 0]
        out_ref[lax.bitwise_xor(mine, 8 + 2 * y)] = x_ref[y, 0]
        out_ref[lax.bitwise_xor(mine, 2 * y + 1)] = c_ref[0, y]
        out_ref[lax.bitwise_xor(mine, 8 + 2 * y + 1)] = c_ref[1, y]
    last = out_ref.shape[0] - 1
    odd = lax.axis_index("box") % 2
    ea_ref[...] = out_ref[(1 - odd) * last]
    eb_ref[...] = out_ref[odd * last]


def codes_by_lane(list_ref, first):
    entry = list_ref[...]
    place = entry - (first + iota(entry.shape, 1)) + REACH
    bits = jnp.where(entry >= 0, lax.shift_left(jnp.ones_like(entry), jnp.maximum(place, 0)), 0)
    row = jnp.sum(bits.astype(F32), axis=0, keepdims=True)
    return jnp.transpose(jnp.broadcast_to(row, (8, row.shape[1])))[:, :1].astype(jnp.int32)


def codes_by_row(list_ref, first):
    entry = list_ref[...]
    place = entry - (first + iota(entry.shape, 0)) + REACH
    bits = jnp.where(entry >= 0, lax.shift_left(jnp.ones_like(entry), jnp.maximum(place, 0)), 0)
    return jnp.sum(bits.astype(F32), axis=1, keepdims=True).astype(jnp.int32)


def masked(code, offset):
    return lax.bitwise_and(code, 1 << (offset + REACH)) != 0


def group_offsets(r):
    return [o for o in OFFSETS if -HALO <= r + o < 2 * HALO]


def translate_kernel(axes, by_row, x_ref, a_ref, b_ref, list_ref, tr_ref, out_ref, f_ref, mt_ref):
    boxes, parts, dirs = x_ref.shape
    half = parts // 2
    first = lax.axis_index(axes[0])
    for name in axes[1:]:
        first = first * lax.axis_size(name) + lax.axis_index(name)
    odd = first % 2
    first = first * boxes
    code = (codes_by_row if by_row else codes_by_lane)(list_ref, first)
    code = jnp.broadcast_to(code, (boxes, 128))
    for k in range(dirs // 128):
        cols = slice(k * 128, (k + 1) * 128)
        for slot, o in enumerate(OFFSETS):
            here = masked(code, o)
            mt_ref[slot, 0, :, cols] = jnp.where(here, tr_ref[slot, 0:1, cols], 0.0)
            mt_ref[slot, 1, :, cols] = jnp.where(here, tr_ref[slot, 1:2, cols], 0.0)
    f_ref[pl.ds((1 - odd) * (HALO + boxes), HALO)] = a_ref[...].astype(F32)
    f_ref[HALO : HALO + boxes] = x_ref[...].astype(F32)
    f_ref[pl.ds(odd * (HALO + boxes), HALO)] = b_ref[...].astype(F32)

    def group(g, cols):
        for r in range(4):
            i = 4 * g + r
            re = jnp.zeros((half, 128), F32)
            im = jnp.zeros((half, 128), F32)
            for o in group_offsets(r):
                slot = OFFSETS.index(o)
                a = mt_ref[slot, 0, i : i + 1, cols]
                b = mt_ref[slot, 1, i : i + 1, cols]
                xr = f_ref[i + HALO + o, :half, cols]
                xi = f_ref[i + HALO + o, half:, cols]
                re = re + (a * xr - b * xi)
                im = im + (a * xi + b * xr)
            out_ref[i, :, cols] = jnp.concatenate([re, im], axis=0).astype(BF16)

    for k in range(dirs // 128):
        cols = slice(k * 128, (k + 1) * 128)

        for g in range(boxes // 4):
            group(g, cols)


def coarse_masks_kernel(list_ref, tr_ref, out_ref):
    boxes = out_ref.shape[2]
    code = jnp.broadcast_to(codes_by_lane(list_ref, 0), (boxes, 128))
    low = iota((1, 128), 1) < 64
    for slot, o in enumerate(OFFSETS):
        here = masked(code, o)
        a = jnp.concatenate([tr_ref[slot, 0:1, :]] * 4, axis=1)
        b = jnp.concatenate([tr_ref[slot, 1:2, :]] * 4, axis=1)
        b = jnp.where(low, -b, b)
        out_ref[slot, 0] = jnp.where(here, a, 0.0)
        out_ref[slot, 1] = jnp.where(here, b, 0.0)


def coarse_translate_kernel(x_ref, mt_ref, out_ref, f_ref, r_ref, y_ref):
    boxes, sub, lanes = x_ref.shape
    zero = jnp.zeros((HALO, sub, lanes), F32)
    for ref in (f_ref, r_ref):
        ref[:HALO] = zero
        ref[HALO + boxes :] = zero
    x = x_ref[...].astype(F32)
    f_ref[HALO : HALO + boxes] = x
    r_ref[HALO : HALO + boxes] = pltpu.roll(x.reshape(boxes * sub, lanes), 64, 1).reshape(x.shape)

    for g in range(boxes // 4):
        for r in range(4):
            i = 4 * g + r
            acc = jnp.zeros((sub, lanes), F32)
            for o in group_offsets(r):
                slot = OFFSETS.index(o)
                a = mt_ref[slot, 0, i : i + 1, :]
                b = mt_ref[slot, 1, i : i + 1, :]
                acc = acc + (a * f_ref[i + HALO + o] + b * r_ref[i + HALO + o])
            y_ref[i * sub : (i + 1) * sub, :] = acc
    for s in range(sub):
        turned = jnp.transpose(y_ref[pl.ds(s, boxes, stride=sub), :])
        for cb in range(4):
            out_ref[8 * cb + s] = turned[32 * cb : 32 * cb + 32, :].astype(BF16)


def near(x):
    return pltpu.with_memory_space_constraint(x, pltpu.VMEM)


def call(body, out, specs, scratch, *args, limit=24 << 20):
    return pl.pallas_call(
        body,
        out_shape=out,
        in_specs=specs,
        out_specs=jax.tree.map(lambda _: VMEM, out),
        scratch_shapes=scratch,
        compiler_params=pltpu.CompilerParams(vmem_limit_bytes=limit),
    )(*args)


def swap(x, axis, bits):
    return lax.ppermute(x, axis, [(i, i ^ bits) for i in range(lax.axis_size(axis))])


def halo(first, second, axes):
    count = lax.axis_size(axes)
    pairs = [(i, i + 1) for i in range(1, count - 1, 2)]
    pairs = pairs + [(b, a) for a, b in pairs]
    a = swap(first, axes, 1)
    return a, lax.ppermute(second, axes, pairs)


def local(
    fine_out,
    fine_list,
    fine_slot,
    fine_translator,
    theta_up_fine,
    phi_up_fine,
    middle_phase,
    middle_list,
    middle_slot,
    middle_translator,
    theta_up_middle,
    phi_up_middle,
    coarse_phase,
    coarse_list,
    coarse_translator,
):
    shape = jax.ShapeDtypeStruct
    boxes, parts, dirs = fine_out.shape
    dir_n = lax.axis_size("dir")
    all_n = dir_n * lax.axis_size("box")
    wide = middle_phase.shape[1]
    widest = coarse_phase.shape[1]
    kids = boxes // 4
    width = wide // dir_n
    piece = (kids, parts, width)
    edge = shape((HALO, parts, dirs), BF16)
    parents, y0, y1, y2, y3, fine_a, fine_b = call(
        middle_kernel,
        (pltpu.VMEM((dir_n,) + piece, BF16),)
        + (pltpu.VMEM((dir_n // 8, 2) + piece, BF16),) * 4
        + (edge, edge),
        [VMEM] * 4 + [SMEM],
        [
            pltpu.VMEM((dirs, wide), BF16),
            pltpu.VMEM((2, boxes, wide), F32),
            pltpu.VMEM((2, boxes * parts, 256), F32),
        ],
        fine_out,
        theta_up_fine.T,
        phi_up_fine.T,
        middle_phase,
        fine_slot,
        limit=60 * 1024 * 1024,
    )
    y1 = swap(y1, "dir", 2)
    y2 = swap(y2, "dir", 4)
    y3 = swap(y3, "dir", 6)
    t2_n = theta_up_middle.shape[0]
    q_n = phi_up_middle.shape[0]
    chunks = call(coarse_kernel,
        pltpu.VMEM((all_n, 8, 128), BF16),
        [VMEM] * 4 + [SMEM],
        [
            pltpu.VMEM((dir_n, kids * parts, 2 * q_n), F32),
            pltpu.VMEM((2, kids, widest), F32),
            pltpu.VMEM((kids, 2, t2_n * 8, 2 * q_n), F32),
        ],
        near(parents),
        theta_up_middle.T,
        phi_up_middle.T,
        coarse_phase,
        middle_slot,
        limit=60 * 1024 * 1024,
    )
    coarse_held = lax.all_to_all(chunks, ALL, split_axis=0, concat_axis=0, tiled=True)
    ys = (y0, y1, y2, y3)
    ys = tuple(near(y) for y in ys)
    xs = call(pack_x_kernel, pltpu.VMEM((4, 2) + piece, BF16), [VMEM] * 4, [], *ys)
    xs = swap(xs, "dir", 8)
    cs = pltpu.VMEM((2, 4) + piece, BF16)
    cs = call(pack_core_kernel, cs, [VMEM] * 5, [], *ys, near(xs))
    cs = swap(cs, "dir", 1)
    edge = shape(piece, BF16)
    middle_out, middle_a, middle_b = call(
        gather_kernel,
        (pltpu.VMEM((dir_n,) + piece, BF16), edge, edge),
        [VMEM] * 6,
        [],
        *ys,
        near(xs),
        near(cs),
    )
    middle_out = middle_out.reshape(dir_n * kids, parts, width)
    fine_a, fine_b = halo(fine_a, fine_b, ALL)
    fine_in = call(
        functools.partial(translate_kernel, ALL, True),
        shape(fine_out.shape, BF16),
        [VMEM] * 5,
        [
            pltpu.VMEM((boxes + 2 * HALO, parts, dirs), F32),
            pltpu.VMEM((12, 2, boxes, dirs), F32),
        ],
        fine_out,
        near(fine_a),
        near(fine_b),
        fine_list,
        fine_translator,
    )
    masks = call(
        coarse_masks_kernel,
        pltpu.VMEM((12, 2, all_n, 128), F32),
        [VMEM] * 2,
        [],
        coarse_list.T,
        coarse_translator,
    )
    middle_a, middle_b = halo(middle_a, middle_b, "box")
    held, _, lanes = middle_out.shape
    middle_in = call(functools.partial(translate_kernel, ("box",), False),
        shape(middle_out.shape, BF16),
        [VMEM] * 5,
        [
            pltpu.VMEM((held + 2 * HALO, parts, lanes), F32),
            pltpu.VMEM((12, 2, held, lanes), F32),
        ],
        near(middle_out),
        near(middle_a),
        near(middle_b),
        middle_list.T,
        middle_translator,
    )
    coarse_in = call(
        coarse_translate_kernel,
        shape((parts, widest // all_n, all_n), BF16),
        [VMEM] * 2,
        [
            pltpu.VMEM((all_n + 2 * HALO, 8, 128), F32),
            pltpu.VMEM((all_n + 2 * HALO, 8, 128), F32),
            pltpu.VMEM((all_n * 8, 128), F32),
        ],
        near(coarse_held),
        near(masks),
    )
    return fine_in, middle_in, jnp.transpose(coarse_in, (2, 0, 1))


def solution(mesh):
    return jax.shard_map(
        local,
        mesh=mesh,
        in_specs=(
            P(ALL, None, None),
            P(ALL, None),
            P("box"),
            P(),
            P(),
            P(),
            P(),
            P("box", None),
            P("box"),
            P(None, None, "dir"),
            P(),
            P(),
            P(),
            P(),
            P(None, None, ALL),
        ),
        out_specs=(P(ALL, None, None), P("box", None, "dir"), P(None, None, ALL)),
        check_vma=False,
    )
```

```python
import jax
import jax.numpy as jnp
from jax import lax
from jax.experimental import pallas as pl
from jax.experimental.pallas import tpu as pltpu
from jax.sharding import PartitionSpec as P


REACH = 7
HALO = 4
ALL = ("box", "dir")
F32 = jnp.float32
BF16 = jnp.bfloat16
OFFSETS = list(range(-REACH, -1)) + list(range(2, REACH + 1))
VMEM = pl.BlockSpec(memory_space=pltpu.VMEM)
ANY = pl.BlockSpec(memory_space=pl.ANY)
SMEM = pl.BlockSpec(memory_space=pltpu.SMEM)


def cos_sin(x):
    y = 0.5 * x
    z = y * y
    s = y * (
        1.0
        + z * (-1 / 6 + z * (1 / 120 + z * (-1 / 5040 + z * (1 / 362880 + z * (-1 / 39916800)))))
    )
    c = 1.0 + z * (
        -0.5
        + z * (1 / 24 + z * (-1 / 720 + z * (1 / 40320 + z * (-1 / 3628800 + z * (1 / 479001600)))))
    )
    return 1.0 - 2.0 * s * s, 2.0 * s * c


def iota(shape, dim):
    return lax.broadcasted_iota(jnp.int32, shape, dim)


def dot(a, b):
    return jnp.dot(a, b, preferred_element_type=F32)


def dot_nt(a, b):
    return lax.dot_general(a, b, (((1,), (1,)), ((), ())), preferred_element_type=F32)


def one_hot(cond):
    return cond.astype(F32).astype(BF16)


def slot_rows(slot_ref, first, count):
    row = iota((count, 128), 0)
    slot = jnp.zeros((count, 128), jnp.int32)
    for b in range(count):
        slot = jnp.where(row == b, slot_ref[first + b], slot)
    return slot


def child_cos_sin(part, slot):
    rows = jnp.broadcast_to(part[3:4, :], slot.shape)
    for j in range(3):
        rows = jnp.where(slot == j, part[j : j + 1, :], rows)
    return cos_sin(rows)


def middle_kernel(
    x_ref,
    theta_ref,
    phi_ref,
    phase_ref,
    slot_ref,
    out_ref,
    keep_ref,
    send_ref,
    ea_ref,
    eb_ref,
    m_ref,
    cs_ref,
    l_ref,
):
    boxes, parts, dirs = x_ref.shape
    t_n, t2_n = theta_ref.shape
    p_n, q_n = phi_ref.shape
    wide = t2_n * q_n
    step = 256
    repeat = one_hot(iota((q_n, step), 1) % q_n == iota((q_n, step), 0))
    phi_row = dot(phi_ref[...], repeat)
    slot = slot_rows(slot_ref, lax.axis_index("dir") * boxes, boxes)
    mine = lax.axis_index("dir")
    core = mine % 2
    ea_ref[...] = x_ref[pl.ds((1 - core) * (boxes - HALO), HALO)]
    eb_ref[...] = x_ref[pl.ds(core * (boxes - HALO), HALO)]
    x = x_ref[...].reshape(boxes * parts, dirs)
    half = parts // 2
    same = jnp.broadcast_to(core, (parts, 128)) == 0

    def prepare(e):
        n = lax.bitwise_xor(mine // 2, e)
        t2 = n * (step // q_n) + iota((t2_n, step), 1) // q_n
        theta_row = dot(theta_ref[...], one_hot(t2 == iota((t2_n, step), 0)))
        for t in range(t_n):
            m_ref[e % 2, t * p_n : (t + 1) * p_n, :] = (theta_row[t : t + 1, :] * phi_row).astype(BF16)
        for k in range(step // 128):
            start = pl.multiple_of(n * step + k * 128, 128)
            cos, sin = child_cos_sin(phase_ref[:, pl.ds(start, 128)], slot)
            cs_ref[e % 2, 0, :, k * 128 : (k + 1) * 128] = cos
            cs_ref[e % 2, 1, :, k * 128 : (k + 1) * 128] = sin

    prepare(0)
    for e in range(wide // step):
        n = lax.bitwise_xor(mine // 2, e)
        l_ref[e % 2] = dot(x, m_ref[e % 2])
        if e + 1 < wide // step:
            prepare(e + 1)
        for p in range(boxes // 4):
            re = jnp.zeros((half, step), F32)
            im = jnp.zeros((half, step), F32)
            for b in range(4 * p, 4 * p + 4):
                c = cs_ref[e % 2, 0, b : b + 1, :]
                s = cs_ref[e % 2, 1, b : b + 1, :]
                lr = l_ref[e % 2, b * parts : b * parts + half, :]
                li = l_ref[e % 2, b * parts + half : (b + 1) * parts, :]
                re = re + (c * lr - s * li)
                im = im + (c * li + s * lr)
            both = jnp.concatenate([re, im], axis=0)
            first = both[:, :128]
            second = both[:, 128:]
            out_ref[2 * n, p] = first.astype(BF16)
            out_ref[2 * n + 1, p] = second.astype(BF16)
            keep_ref[e, p] = jnp.where(same, first, second).astype(BF16)
            send_ref[e, p] = jnp.where(same, second, first).astype(BF16)


def coarse_kernel(
    par_ref, theta_ref, phi_ref, phase_ref, slot_ref, out_ref, a_ref, cs_ref, l_ref, v_ref
):
    blocks, kids, parts, lanes = par_ref.shape
    t_n, t2_n = theta_ref.shape
    p_n, q_n = phi_ref.shape
    pair = lanes // p_n
    tall = one_hot(iota((lanes, p_n), 0) % p_n == iota((lanes, p_n), 1))
    phi_tall = dot(tall, phi_ref[...])
    w = jnp.concatenate(
        [jnp.where(iota((lanes, q_n), 0) // p_n == h, phi_tall, 0.0) for h in range(pair)], axis=1
    ).astype(BF16)
    e1 = one_hot(iota((t2_n * 8, t2_n), 0) // 8 == iota((t2_n * 8, t2_n), 1))
    e2 = one_hot(iota((t_n, t_n * 8), 1) // 8 == iota((t_n, t_n * 8), 0))
    stretched = dot(dot_nt(e1, theta_ref[...]).astype(BF16), e2)
    same = iota(stretched.shape, 0) % 8 == iota(stretched.shape, 1) % 8
    k8 = jnp.where(same, stretched, 0.0).astype(BF16)
    rows = kids * parts
    slot = slot_rows(slot_ref, lax.axis_index("dir") * kids, kids)
    for d in range(blocks):
        a_ref[d] = dot(par_ref[d].reshape(rows, lanes), w)
        for t2 in range(d * t2_n // blocks, (d + 1) * t2_n // blocks):
            cols = slice(t2 * q_n, (t2 + 1) * q_n)
            cos, sin = child_cos_sin(phase_ref[:, cols], slot)
            cs_ref[0, :, cols] = cos
            cs_ref[1, :, cols] = sin

    def lift(m, a):
        cols = []
        for r in (m * parts + 8 * a, m * parts + 16 + 8 * a):
            pieces = [
                a_ref[t // pair, r : r + 8, (t % pair) * q_n : (t % pair + 1) * q_n]
                for t in range(t_n)
            ]
            cols.append(jnp.concatenate(pieces, axis=0).astype(BF16))
        l_ref[m, a] = dot(k8, jnp.concatenate(cols, axis=1))

    def combine(t2, a):
        cols = slice(t2 * q_n, (t2 + 1) * q_n)
        re = jnp.zeros((8, q_n), F32)
        im = jnp.zeros((8, q_n), F32)
        for m in range(kids):
            c = cs_ref[0, m : m + 1, cols]
            s = cs_ref[1, m : m + 1, cols]
            lr = l_ref[m, a, t2 * 8 : t2 * 8 + 8, :q_n]
            li = l_ref[m, a, t2 * 8 : t2 * 8 + 8, q_n:]
            re = re + (c * lr - s * li)
            im = im + (c * li + s * lr)
        return re, im

    for m in range(kids):
        lift(m, 0)
    for m in range(kids):
        lift(m, 1)
        for t2 in range(m * t2_n // kids, (m + 1) * t2_n // kids):
            v_ref[t2, 0], v_ref[t2, 1] = combine(t2, 0)
    lane = iota((8, q_n), 1)
    low = lane < 64
    even = lane % 64 < 32
    for t2 in range(t2_n):
        v = {(0, 0): v_ref[t2, 0], (1, 0): v_ref[t2, 1]}
        v[0, 1], v[1, 1] = combine(t2, 1)
        u = {}
        for a in range(2):
            u[0, a] = jnp.where(low, v[0, a], pltpu.roll(v[1, a], 64, 1))
            u[1, a] = jnp.where(low, pltpu.roll(v[0, a], 64, 1), v[1, a])
        for h in range(2):
            out_ref[t2 * 4 + 2 * h] = jnp.where(even, u[h, 0], pltpu.roll(u[h, 1], 32, 1)).astype(BF16)
            out_ref[t2 * 4 + 2 * h + 1] = jnp.where(
                even, pltpu.roll(u[h, 0], 96, 1), u[h, 1]
            ).astype(BF16)


def pack_x_kernel(own_ref, other_ref, out_ref):
    for core, ref in enumerate((own_ref, other_ref)):
        out_ref[core] = ref[4:]


def pack_y_kernel(own_ref, other_ref, x_ref, *out_refs):
    for y, ref in enumerate(out_refs):
        ref[0, 0] = own_ref[y + 1]
        ref[0, 1] = other_ref[y + 1]
        ref[1, 0] = x_ref[0, y + 1]
        ref[1, 1] = x_ref[1, y + 1]


def gather_kernel(
    own_ref, other_ref, x_ref, y1_ref, y2_ref, y3_ref, out_ref, ea_ref, eb_ref
):
    mine = lax.axis_index("dir")
    out_ref[mine] = own_ref[0]
    out_ref[lax.bitwise_xor(mine, 1)] = other_ref[0]
    out_ref[lax.bitwise_xor(mine, 8)] = x_ref[0, 0]
    out_ref[lax.bitwise_xor(mine, 9)] = x_ref[1, 0]
    for y, ref in enumerate((y1_ref, y2_ref, y3_ref)):
        for x in range(2):
            for core in range(2):
                out_ref[lax.bitwise_xor(mine, 8 * x + 2 * (y + 1) + core)] = ref[x, core]
    last = out_ref.shape[0] - 1
    odd = lax.axis_index("box") % 2
    ea_ref[...] = out_ref[(1 - odd) * last]
    eb_ref[...] = out_ref[odd * last]


def codes_by_lane(list_ref, first):
    entry = list_ref[...]
    place = entry - (first + iota(entry.shape, 1)) + REACH
    bits = jnp.where(entry >= 0, lax.shift_left(jnp.ones_like(entry), jnp.maximum(place, 0)), 0)
    row = jnp.sum(bits.astype(F32), axis=0, keepdims=True)
    return jnp.transpose(jnp.broadcast_to(row, (8, row.shape[1])))[:, :1].astype(jnp.int32)


def codes_by_row(list_ref, first):
    entry = list_ref[...]
    place = entry - (first + iota(entry.shape, 0)) + REACH
    bits = jnp.where(entry >= 0, lax.shift_left(jnp.ones_like(entry), jnp.maximum(place, 0)), 0)
    return jnp.sum(bits.astype(F32), axis=1, keepdims=True).astype(jnp.int32)


def masked(code, offset):
    return lax.bitwise_and(code, 1 << (offset + REACH)) != 0


def group_offsets(r):
    return [o for o in OFFSETS if -HALO <= r + o < 2 * HALO]


def fill_masks(mt_ref, tr_ref, code):
    boxes, dirs = mt_ref.shape[2:]
    code = jnp.broadcast_to(code, (boxes, 128))
    for k in range(dirs // 128):
        cols = slice(k * 128, (k + 1) * 128)
        for slot, o in enumerate(OFFSETS):
            here = masked(code, o)
            mt_ref[slot, 0, :, cols] = jnp.where(here, tr_ref[slot, 0:1, cols], 0.0)
            mt_ref[slot, 1, :, cols] = jnp.where(here, tr_ref[slot, 1:2, cols], 0.0)


def translate_groups(f_ref, mt_ref, out_ref, groups, start):
    half, dirs = f_ref.shape[1] // 2, f_ref.shape[2]
    for k in range(dirs // 128):
        cols = slice(k * 128, (k + 1) * 128)
        for i in [4 * g + r for g in groups for r in range(4)]:
            re = jnp.zeros((half, 128), F32)
            im = jnp.zeros((half, 128), F32)
            for o in group_offsets(i % 4):
                slot = OFFSETS.index(o)
                a = mt_ref[slot, 0, i : i + 1, cols]
                b = mt_ref[slot, 1, i : i + 1, cols]
                xr = f_ref[i + HALO + o, :half, cols]
                xi = f_ref[i + HALO + o, half:, cols]
                re = re + (a * xr - b * xi)
                im = im + (a * xi + b * xr)
            out_ref[i - start, :, cols] = jnp.concatenate([re, im], axis=0).astype(BF16)


def place_edges(f_ref, a_ref, b_ref, odd):
    far = f_ref.shape[0] - HALO
    f_ref[pl.ds((1 - odd) * far, HALO)] = a_ref[...].astype(F32)
    f_ref[pl.ds(odd * far, HALO)] = b_ref[...].astype(F32)


def fine_inner_kernel(x_any, list_ref, tr_ref, inner_ref, copy_ref, mt_ref, sem, f_ref):
    fetch = pltpu.make_async_copy(x_any, copy_ref, sem)
    fetch.start()
    boxes = copy_ref.shape[0]
    first = lax.axis_index("box") * lax.axis_size("dir") + lax.axis_index("dir")
    fill_masks(mt_ref, tr_ref, codes_by_row(list_ref, first * boxes))
    fetch.wait()
    f_ref[HALO : HALO + boxes] = copy_ref[...].astype(F32)
    translate_groups(f_ref, mt_ref, inner_ref, range(1, boxes // 4 - 1), 4)


def fine_outer_kernel(inner_ref, x_ref, mt_ref, a_ref, b_ref, out_ref, f_ref):
    boxes = x_ref.shape[0]
    place_edges(f_ref, a_ref, b_ref, lax.axis_index("dir") % 2)
    f_ref[HALO : HALO + boxes] = x_ref[...].astype(F32)
    out_ref[4 : boxes - 4] = inner_ref[...]
    translate_groups(f_ref, mt_ref, out_ref, (0, boxes // 4 - 1), 0)


def middle_masks_kernel(list_ref, tr_ref, mt_ref):
    boxes = mt_ref.shape[2]
    fill_masks(mt_ref, tr_ref, codes_by_lane(list_ref, lax.axis_index("box") * boxes))


def middle_translate_kernel(x_ref, a_ref, b_ref, mt_ref, out_ref, f_ref):
    boxes = x_ref.shape[0]
    place_edges(f_ref, a_ref, b_ref, lax.axis_index("box") % 2)
    f_ref[HALO : HALO + boxes] = x_ref[...].astype(F32)
    translate_groups(f_ref, mt_ref, out_ref, range(boxes // 4), 0)


def coarse_masks_kernel(list_ref, tr_ref, out_ref):
    boxes = out_ref.shape[2]
    code = jnp.broadcast_to(codes_by_lane(list_ref, 0), (boxes, 128))
    low = iota((1, 128), 1) < 64
    for slot, o in enumerate(OFFSETS):
        here = masked(code, o)
        a = jnp.concatenate([tr_ref[slot, 0:1, :]] * 4, axis=1)
        b = jnp.concatenate([tr_ref[slot, 1:2, :]] * 4, axis=1)
        b = jnp.where(low, -b, b)
        out_ref[slot, 0] = jnp.where(here, a, 0.0)
        out_ref[slot, 1] = jnp.where(here, b, 0.0)


def coarse_translate_kernel(
    x_any, mt_ref, out_any, x_ref, o_ref, in_sem, out_sem, f_ref, r_ref, y_ref
):
    boxes, sub, lanes = x_ref.shape
    chunks = in_sem.shape[0]
    size = boxes // chunks
    fetches = []
    for q in range(chunks):
        part = pl.ds(q * size, size)
        fetches.append(pltpu.make_async_copy(x_any.at[part], x_ref.at[part], in_sem.at[q]))
        fetches[q].start()
    zero = jnp.zeros((HALO, sub, lanes), F32)
    for ref in (f_ref, r_ref):
        ref[:HALO] = zero
        ref[HALO + boxes :] = zero

    def group(g):
        for r in range(4):
            i = 4 * g + r
            acc = jnp.zeros((sub, lanes), F32)
            for o in group_offsets(r):
                slot = OFFSETS.index(o)
                a = mt_ref[slot, 0, i : i + 1, :]
                b = mt_ref[slot, 1, i : i + 1, :]
                acc = acc + (a * f_ref[i + HALO + o] + b * r_ref[i + HALO + o])
            y_ref[i * sub : (i + 1) * sub, :] = acc

    stores = []

    def finish(h):
        for s in range(sub):
            turned = jnp.transpose(y_ref[pl.ds(h * lanes * sub + s, lanes, stride=sub), :])
            for cb in range(4):
                o_ref[h, 8 * cb + s] = turned[32 * cb : 32 * cb + 32, :].astype(BF16)
        target = out_any.at[:, :, pl.ds(h * lanes, lanes)]
        stores.append(pltpu.make_async_copy(o_ref.at[h], target, out_sem.at[h]))
        stores[h].start()

    done = 0
    for q in range(chunks):
        fetches[q].wait()
        x = x_ref[q * size : (q + 1) * size].astype(F32)
        here = slice(HALO + q * size, HALO + (q + 1) * size)
        f_ref[here] = x
        r_ref[here] = pltpu.roll(x.reshape(size * sub, lanes), 64, 1).reshape(x.shape)
        upto = boxes // 4 if q + 1 == chunks else (q + 1) * size // 4 - 1
        for g in range(done, upto):
            group(g)
            if (4 * g + 4) % lanes == 0:
                finish((4 * g + 4) // lanes - 1)
        done = upto
    for copy in stores:
        copy.wait()


def near(x):
    return pltpu.with_memory_space_constraint(x, pltpu.VMEM)


def call(body, out, specs, scratch, *args, limit=24 << 20, out_space=VMEM):
    return pl.pallas_call(
        body,
        out_shape=out,
        in_specs=specs,
        out_specs=jax.tree.map(lambda _: out_space, out),
        scratch_shapes=scratch,
        compiler_params=pltpu.CompilerParams(vmem_limit_bytes=limit),
    )(*args)


def swap(x, axis, bits):
    return lax.ppermute(x, axis, [(i, i ^ bits) for i in range(lax.axis_size(axis))])


def halo(first, second, axes):
    count = lax.axis_size(axes)
    pairs = [(i, i + 1) for i in range(1, count - 1, 2)]
    pairs = pairs + [(b, a) for a, b in pairs]
    a = swap(first, axes, 1)
    return a, lax.ppermute(second, axes, pairs)


def local(
    fine_out,
    fine_list,
    fine_slot,
    fine_translator,
    theta_up_fine,
    phi_up_fine,
    middle_phase,
    middle_list,
    middle_slot,
    middle_translator,
    theta_up_middle,
    phi_up_middle,
    coarse_phase,
    coarse_list,
    coarse_translator,
):
    shape = jax.ShapeDtypeStruct
    boxes, parts, dirs = fine_out.shape
    dir_n = lax.axis_size("dir")
    all_n = dir_n * lax.axis_size("box")
    wide = middle_phase.shape[1]
    widest = coarse_phase.shape[1]
    kids = boxes // 4
    width = wide // dir_n
    piece = (kids, parts, width)
    edge = shape((HALO, parts, dirs), BF16)
    parents, own, other, fine_a, fine_b = call(
        middle_kernel,
        (pltpu.VMEM((dir_n,) + piece, BF16),)
        + (pltpu.VMEM((dir_n // 2,) + piece, BF16),) * 2
        + (edge, edge),
        [VMEM] * 4 + [SMEM],
        [
            pltpu.VMEM((2, dirs, 256), BF16),
            pltpu.VMEM((2, 2, boxes, 256), F32),
            pltpu.VMEM((2, boxes * parts, 256), F32),
        ],
        fine_out,
        theta_up_fine.T,
        phi_up_fine.T,
        middle_phase,
        fine_slot,
        limit=60 * 1024 * 1024,
    )
    own = near(own)
    other = near(swap(other, "dir", 1))
    xs = pltpu.VMEM((2, dir_n // 4) + piece, BF16)
    xs = call(pack_x_kernel, xs, [VMEM] * 2, [], own, other)
    xs = near(swap(xs, "dir", 8))
    t2_n = theta_up_middle.shape[0]
    q_n = phi_up_middle.shape[0]
    chunks = call(coarse_kernel,
        pltpu.VMEM((all_n, 8, 128), BF16),
        [VMEM] * 4 + [SMEM],
        [
            pltpu.VMEM((dir_n, kids * parts, 2 * q_n), F32),
            pltpu.VMEM((2, kids, widest), F32),
            pltpu.VMEM((kids, 2, t2_n * 8, 2 * q_n), F32),
            pltpu.VMEM((t2_n, 2, 8, q_n), F32),
        ],
        near(parents),
        theta_up_middle.T,
        phi_up_middle.T,
        coarse_phase,
        middle_slot,
        limit=60 * 1024 * 1024,
    )
    coarse_held = lax.all_to_all(chunks, ALL, split_axis=0, concat_axis=0, tiled=True)
    ys = (pltpu.VMEM((2, 2) + piece, BF16),) * 3
    ys = call(pack_y_kernel, ys, [VMEM] * 3, [], own, other, xs)
    ys = tuple(near(swap(y, "dir", bits)) for y, bits in zip(ys, (2, 4, 6)))
    edge = shape(piece, BF16)
    middle_out, middle_a, middle_b = call(
        gather_kernel,
        (pltpu.VMEM((dir_n,) + piece, BF16), edge, edge),
        [VMEM] * 6,
        [],
        own,
        other,
        xs,
        *ys,
    )
    middle_out = middle_out.reshape(dir_n * kids, parts, width)
    fine_a, fine_b = halo(fine_a, fine_b, ALL)
    inner, fine_copy, fine_masks = call(
        fine_inner_kernel,
        (
            pltpu.VMEM((boxes - 8, parts, dirs), BF16),
            pltpu.VMEM(fine_out.shape, BF16),
            pltpu.VMEM((12, 2, boxes, dirs), F32),
        ),
        [ANY] + [VMEM] * 2,
        [pltpu.SemaphoreType.DMA(()), pltpu.VMEM((boxes + 2 * HALO, parts, dirs), F32)],
        pltpu.with_memory_space_constraint(fine_out, pltpu.HBM),
        fine_list,
        fine_translator,
    )
    fine_in = call(
        fine_outer_kernel,
        shape(fine_out.shape, BF16),
        [VMEM] * 5,
        [pltpu.VMEM((boxes + 2 * HALO, parts, dirs), F32)],
        near(inner),
        near(fine_copy),
        near(fine_masks),
        near(fine_a),
        near(fine_b),
    )
    masks = call(
        coarse_masks_kernel,
        pltpu.VMEM((12, 2, all_n, 128), F32),
        [VMEM] * 2,
        [],
        coarse_list.T,
        coarse_translator,
    )
    middle_a, middle_b = halo(middle_a, middle_b, "box")
    held, _, lanes = middle_out.shape
    middle_masks = call(
        middle_masks_kernel,
        pltpu.VMEM((12, 2, held, lanes), F32),
        [VMEM] * 2,
        [],
        middle_list.T,
        middle_translator,
    )
    middle_in = call(
        middle_translate_kernel,
        shape(middle_out.shape, BF16),
        [VMEM] * 4,
        [pltpu.VMEM((held + 2 * HALO, parts, lanes), F32)],
        near(middle_out),
        near(middle_a),
        near(middle_b),
        near(middle_masks),
    )
    coarse_in = call(
        coarse_translate_kernel,
        shape((parts, widest // all_n, all_n), BF16),
        [ANY, VMEM],
        [
            pltpu.VMEM((all_n, 8, 128), BF16),
            pltpu.VMEM((all_n // 128, parts, widest // all_n, 128), BF16),
            pltpu.SemaphoreType.DMA((4,)),
            pltpu.SemaphoreType.DMA((all_n // 128,)),
            pltpu.VMEM((all_n + 2 * HALO, 8, 128), F32),
            pltpu.VMEM((all_n + 2 * HALO, 8, 128), F32),
            pltpu.VMEM((all_n * 8, 128), F32),
        ],
        coarse_held,
        near(masks),
        out_space=ANY,
    )
    return fine_in, middle_in, jnp.transpose(coarse_in, (2, 0, 1))


def solution(mesh):
    return jax.shard_map(
        local,
        mesh=mesh,
        in_specs=(
            P(ALL, None, None),
            P(ALL, None),
            P("box"),
            P(),
            P(),
            P(),
            P(),
            P("box", None),
            P("box"),
            P(None, None, "dir"),
            P(),
            P(),
            P(),
            P(),
            P(None, None, ALL),
        ),
        out_specs=(P(ALL, None, None), P("box", None, "dir"), P(None, None, ALL)),
        check_vma=False,
    )
```
